256 devices in a mesh: space: 32 (over x, z), col: 8 (over y, core).
Axes of the slice: x: 4, y: 4, z: 8, core: 2. Of those that a mesh axis runs over, the one named last changes fastest.
Arguments:
- blocks: bfloat16 [2560, 24, 128, 128], P('space', 'col'), may hold values from -0.109375 to 0.109375
- basis_tiles: bfloat16 [2560, 128, 128], P('space'), may hold values from -6 to 6
- weights: float32 [2560, 128], P('space'), may hold values from 0.1 to 1
- neighbour_device: int32 [2560, 24], P('space', 'col'), may hold values from 0 to 31, as said below
- neighbour_row: int32 [2560, 24], P('space', 'col'), may hold values from 0 to 79
- counts: int32 [2560], P('space'), may hold values from 12 to 24
- aggregate: int32 [2560], P('space'), may hold values from 0 to 9
- pair_slot: int32 [2560, 24], P('space', 'col'), may hold values from 0 to 3
Outputs:
- coarse: float32 [1280, 128, 128], P(('space', 'col'))
The draws below stay inside these ranges and needn't reach their ends.
Inputs may be any that keep to these rules, and one draw needn't show every extreme that they name: `neighbour_device`: among the slots of one device's 80 rows that fall to one index of col, exactly 60 name another device; no other device is named more than 3 times there, and some other device exactly 3 times.
All inputs are finite; a program needn't handle non-finite values.
Results may differ from the reference program's by a relative error of at most 0.0045.
Values may be sent and summed in bfloat16 or wider, within the bound.
A program may use at most 128 MiB of HBM per device.

```python
import math
import jax
import jax.numpy as jnp
from jax import lax

BS = 128
CB = 128
K = 24
KC = 4
CAP = 3
RB = 80
NCD = 10
REMOTE = 60
NB = 2560
N_SPACE = 32
N_COL = 8


def draw_neighbour_device(key, part):
    slot_count = K // N_COL
    slot_total = RB * slot_count

    def draw_group(space_pos, col_pos):
        group_key = jax.random.fold_in(jax.random.fold_in(jax.random.fold_in(key, 7), space_pos), col_pos)
        key_pool, key_order = jax.random.split(group_key)
        others = (space_pos + 2 + jnp.arange((N_SPACE - 2) * CAP, dtype=jnp.int32) // CAP) % N_SPACE
        others = jax.random.permutation(key_pool, others)
        successor = jnp.full((CAP,), (space_pos + 1) % N_SPACE, jnp.int32)
        own_slots = jnp.full((slot_total - REMOTE,), space_pos, jnp.int32)
        peer_list = jnp.concatenate([successor, others[:REMOTE - CAP], own_slots])
        peer_list = jax.random.permutation(key_order, peer_list)
        return peer_list.reshape(RB, slot_count)
    space_range = jnp.arange(N_SPACE, dtype=jnp.int32)
    col_range = jnp.arange(N_COL, dtype=jnp.int32)
    grouped = jax.vmap(jax.vmap(draw_group, (None, 0)), (0, None))(space_range, col_range)
    return jnp.transpose(grouped, (0, 2, 1, 3)).reshape(N_SPACE * RB, K).astype(jnp.int32)


def set_ends(array, key, least, largest):
    longest = array.shape.index(max(array.shape))
    spots = []
    for shift in (0, 1):
        where = [jax.random.randint(jax.random.fold_in(key, axis), (), 0, length) for axis, length in enumerate(array.shape)]
        where[longest] = (where[longest] + shift) % array.shape[longest]
        spots.append(tuple(where))
    return array.at[spots[0]].set(least).at[spots[1]].set(largest)


def block_scale(key, dims, cuts, smallest, high):
    def one(axis_at, blocks):
        draws = jax.random.uniform(jax.random.fold_in(jax.random.fold_in(key, 6), axis_at), (blocks,), jnp.float32, smallest / len(cuts), high / len(cuts))
        return jnp.repeat(jnp.exp(draws), dims[axis_at] // blocks).reshape((-1,) + (1,) * (len(dims) - axis_at - 1))

    factor_of = one(*cuts[0])
    for cut in cuts[1:]:
        factor_of = factor_of * one(*cut)
    return factor_of


def noise(key, shape, width, most, shards=(), kind=jnp.bfloat16):
    loudness = block_scale(key, shape, shards, -0.22, 0.18) if shards else 1.0
    values = jax.random.normal(key, shape, jnp.float32) * width * loudness
    return jnp.minimum(jnp.maximum(values, -most), most).astype(kind)


def setup_inputs(seed: int = 0) -> dict:
    key_of = jax.random.split(jax.random.key(seed), 9)
    return {
        "blocks": noise(key_of[0], (NB, K, BS, BS), (BS * K) ** -0.5, 0.109375, ((0, 32), (1, 8))),
        "basis_tiles": noise(key_of[1], (NB, BS, CB), 1.0, 6.0, ((0, 32),)),
        "weights": jnp.clip(jnp.exp(math.log(1.0) - 2.3025851 * jax.random.uniform(key_of[2], (NB, BS), jnp.float32) ** block_scale(key_of[2], (NB, BS), ((0, 32),), -0.2, 0.2)), 0.1, 1.0),
        "neighbour_device": draw_neighbour_device(jax.random.fold_in(key_of[8], 71), 0),
        "neighbour_row": set_ends(jax.random.randint(key_of[4], (NB, K), 0, RB), jax.random.fold_in(key_of[4], 1), 0, RB - 1).astype(jnp.int32),
        "counts": set_ends(jax.random.randint(key_of[5], (NB,), K // 2, K + 1), jax.random.fold_in(key_of[5], 1), K // 2, K).astype(jnp.int32),
        "aggregate": set_ends(jax.random.randint(key_of[6], (NB,), 0, NCD), jax.random.fold_in(key_of[6], 1), 0, NCD - 1).astype(jnp.int32),
        "pair_slot": set_ends(jax.random.randint(key_of[7], (NB, K), 0, KC), jax.random.fold_in(key_of[7], 1), 0, KC - 1).astype(jnp.int32),
    }


def reference(blocks, basis_tiles, weights, neighbour_device, neighbour_row, counts, aggregate, pair_slot):
    neighbour_id = (neighbour_device * RB + neighbour_row).astype(jnp.int32)
    usable = jnp.arange(K, dtype=jnp.int32)[None, :] < counts[:, None]
    masked = jnp.where(usable[:, :, None, None], blocks, jnp.zeros((), blocks.dtype))
    masked_group = masked.reshape(N_SPACE, RB, K, BS, BS)
    id_group = neighbour_id.reshape(N_SPACE, RB, K)

    def smooth(pieces):
        block_group, neighbour_ids = pieces
        fetched = basis_tiles[neighbour_ids].astype(jnp.float32)
        return jnp.einsum("rkab,rkbc->rac", block_group.astype(jnp.float32), fetched)

    smoothed = lax.map(smooth, (masked_group, id_group)).reshape(N_SPACE * RB, BS, CB)
    prolong = (basis_tiles.astype(jnp.float32) - weights[:, :, None] * smoothed).astype(jnp.bfloat16)
    targets = (aggregate[:, None] * KC + pair_slot).astype(jnp.int32)

    def galerkin(pieces):
        block_group, neighbour_ids, own_tiles, target_group = pieces
        fetched = prolong[neighbour_ids].astype(jnp.float32)
        applied = jnp.einsum("rkab,rkbc->rkac", block_group.astype(jnp.float32), fetched).astype(jnp.bfloat16)
        contribution = jnp.einsum("rad,rkae->rkde", own_tiles.astype(jnp.float32), applied.astype(jnp.float32))
        return jax.ops.segment_sum(contribution.reshape(RB * K, CB, CB), target_group.reshape(RB * K), num_segments=NCD * KC)

    coarse = lax.map(galerkin, (masked_group, id_group, prolong.reshape(N_SPACE, RB, BS, CB), targets.reshape(N_SPACE, RB, K)))
    return coarse.reshape(N_SPACE * NCD * KC, CB, CB)
```

```python
import functools

import jax
import jax.numpy as jnp
from jax import lax
from jax.experimental import pallas as pl
from jax.experimental.pallas import tpu as pltpu
from jax.sharding import PartitionSpec as P

KC = 4
CAP = 3
NCD = 10
NX, NZ, NY = 4, 8, 4
MESH = pl.DeviceIdType.MESH
F32 = jnp.float32
BF16 = jnp.bfloat16


def dot(a, b):
    return jnp.dot(a, b, preferred_element_type=F32)


def dot_t(a, b):
    return lax.dot_general(a, b, (((0,), (0,)), ((), ())), preferred_element_type=F32)


def step_offset(o):
    zi, xi = o // NX, o % NX
    hz, hx = (zi + 1) // 2, (xi + 1) // 2
    dz = ((zi % 2) * hz + (1 - zi % 2) * (NZ - hz)) % NZ
    dx = ((xi % 2) * hx + (1 - xi % 2) * (NX - hx)) % NX
    return dx, dz


def kernel(
    sizes,
    tab,
    req,
    weights,
    blocks_hbm,
    basis_hbm,
    out,
    blocks,
    basis,
    ptab,
    asked_v,
    asked,
    stage,
    recv1,
    recv2,
    big,
    total,
    xs,
    xr,
    s1,
    r1,
    s2,
    r2,
    xs_f,
    xr_f,
    s1_f,
    r1_f,
    s2_f,
    r2_f,
    load_sem,
    req_send,
    req_recv,
    a_send,
    a_recv,
    b_send,
    b_recv,
    rs_send,
    rs_recv,
    rf_send,
    rf_recv,
    ag_send,
    ag_recv,
):
    rows, slots, n_local = sizes
    space_count = NX * NZ
    peers = space_count - 1
    own_rows = rows // (2 * NY)
    lidx_at, ridx_at = 0, slots
    slot_at = 2 * slots
    loc_at = slot_at + space_count * CAP
    rem_at = loc_at + n_local
    n_remote = slots - n_local
    last_l_at = rem_at + n_remote
    last_r_at = last_l_at + NCD * KC
    r_base = rows
    c_base = n_local
    g_base = n_local + space_count * CAP

    me = lax.axis_index("space")
    col = lax.axis_index("col")
    mx, mz = me // NZ, me % NZ
    my, core = col // 2, col % 2
    ya = my + 1 - 2 * (my % 2)
    yb = NY - 1 - my
    yo = (my + 2) % NY
    dev_x = (me, my * 2 + 1 - core)
    dev_a = (me, ya * 2 + core)
    dev_b = (me, yb * 2 + core)

    def target(o):
        dx, dz = step_offset(o)
        return (((mx + dx) % NX) * NZ + (mz + dz) % NZ, col)

    def origin(o):
        dx, dz = step_offset(o)
        return (((mx + NX - dx) % NX) * NZ + (mz + NZ - dz) % NZ, col)

    load_a = pltpu.make_async_copy(blocks_hbm, blocks, load_sem.at[0])
    load_b = pltpu.make_async_copy(basis_hbm, basis.at[pl.ds(0, rows)], load_sem.at[1])
    load_b.start()
    load_a.start()

    barrier = pltpu.get_barrier_semaphore()

    def greet(o, carry):
        pl.semaphore_signal(barrier, 1, device_id=target(o), device_id_type=MESH)
        return carry

    lax.fori_loop(1, space_count, greet, 0)
    for peer in (dev_x, dev_a, dev_b):
        pl.semaphore_signal(barrier, 1, device_id=peer, device_id_type=MESH)
    zero_b = jnp.zeros((128, 128), BF16)
    zero_f = jnp.zeros((128, 128), F32)
    basis[rows] = zero_b
    ptab[rows] = zero_b
    big[r_base] = zero_f
    big[c_base] = zero_f
    pl.semaphore_wait(barrier, peers + 3)

    def remote(src, dst, send, recv, dev):
        return pltpu.make_async_remote_copy(
            src, dst, send, recv, device_id=dev, device_id_type=MESH
        )

    def ask(o):
        return remote(req.at[o], asked_v.at[o], req_send.at[o], req_recv.at[o], origin(o))

    def ask_start(o, carry):
        ask(o).start()
        return carry

    lax.fori_loop(1, space_count, ask_start, 0)

    def ask_wait(o, carry):
        ask(o).wait()
        return carry

    lax.fori_loop(1, space_count, ask_wait, 0)
    to_scalar = pltpu.make_async_copy(
        asked_v.at[pl.ds(1, peers)], asked.at[pl.ds(1, peers)], load_sem.at[2]
    )
    to_scalar.start()
    to_scalar.wait()
    load_b.wait()

    def halo1(o):
        return remote(stage.at[o], recv1.at[o], a_send.at[o], a_recv.at[o], target(o))

    def halo2(o):
        return remote(stage.at[o], recv2.at[o], b_send.at[o], b_recv.at[o], target(o))

    def send1(o, carry):
        for j in range(CAP):
            stage[o, j] = basis[asked[o, 0, j]]
        halo1(o).start()
        return carry

    lax.fori_loop(1, space_count, send1, 0)
    load_a.wait()

    def local_smooth(i, carry):
        lhs = jnp.concatenate([blocks[3 * i + k] for k in range(3)], axis=1)
        rhs = jnp.concatenate([basis[tab[lidx_at + 3 * i + k]] for k in range(3)], axis=0)
        big[i] = dot(lhs, rhs)
        return carry

    lax.fori_loop(0, rows, local_smooth, 0, unroll=2)

    def remote_smooth(o, carry):
        halo1(o).wait_recv()
        for j in range(CAP):
            big[r_base + o * CAP + j] = dot(blocks[tab[slot_at + o * CAP + j]], recv1[o, j])
        return carry

    lax.fori_loop(1, space_count, remote_smooth, 0)

    def reduce_scatter(n, part, xs, xr, s1, r1, s2, r2, send, recv):
        groups = (ya, yb, yo, my)
        h1 = (n + 1) // 2
        h2 = n - h1

        def swap(i):
            return remote(
                xs.at[pl.ds(i * n, n)], xr.at[pl.ds(i * n, n)], send.at[i], recv.at[i], dev_x
            )

        for i in range(4):

            def fill(t, carry):
                xs[i * n + t] = part((groups[i] * 2 + 1 - core) * n + t).astype(BF16)
                return carry

            lax.fori_loop(0, n, fill, 0)
            swap(i).start()
        for i in range(4):

            def keep(t, carry):
                total[i * n + t] = part((groups[i] * 2 + core) * n + t)
                return carry

            lax.fori_loop(0, n, keep, 0)

        def hop(src, dst, at, size, sem, dev):
            return remote(
                src.at[pl.ds(at, size)], dst.at[pl.ds(at, size)], send.at[sem], recv.at[sem], dev
            )

        m0 = hop(s1, r1, 0, h1, 4, dev_a)
        m1 = hop(s1, r1, h1, h1, 5, dev_a)
        m2 = hop(s1, r1, 2 * h1, h2, 6, dev_b)
        m3 = hop(s1, r1, 2 * h1 + h2, h2, 7, dev_b)
        m4 = hop(s2, r2, 0, h1, 8, dev_b)
        m5 = hop(s2, r2, h1, h2, 9, dev_a)

        def add_swapped(i):
            swap(i).wait_recv()

            def add(t, carry):
                total[i * n + t] += xr[i * n + t].astype(F32)
                return carry

            lax.fori_loop(0, n, add, 0)

        def put(dst, at, first, size):
            def one(t, carry):
                dst[at + t] = total[first + t].astype(BF16)
                return carry

            lax.fori_loop(0, size, one, 0)

        def take(src, at, first, size):
            def one(t, carry):
                total[first + t] += src[at + t].astype(F32)
                return carry

            lax.fori_loop(0, size, one, 0)

        add_swapped(0)
        put(s1, 0, 0, h1)
        m0.start()
        add_swapped(1)
        put(s1, 2 * h1, n + h1, h2)
        m2.start()
        add_swapped(2)
        put(s1, h1, 2 * n, h1)
        m1.start()
        put(s1, 2 * h1 + h2, 2 * n + h1, h2)
        m3.start()
        add_swapped(3)
        m1.wait_recv()
        take(r1, h1, n, h1)
        put(s2, 0, n, h1)
        m4.start()
        m3.wait_recv()
        take(r1, 2 * h1 + h2, h1, h2)
        put(s2, h1, h1, h2)
        m5.start()
        m0.wait_recv()
        take(r1, 0, 3 * n, h1)
        m2.wait_recv()
        take(r1, 2 * h1, 3 * n + h1, h2)
        m4.wait_recv()
        take(r2, 0, 3 * n, h1)
        m5.wait_recv()
        take(r2, h1, 3 * n + h1, h2)

        def drain():
            for i in range(4):
                swap(i).wait_send()
            for m in (m0, m1, m2, m3, m4, m5):
                m.wait_send()

        return drain

    def smooth_part(row):
        acc = big[row]
        for k in range(3):
            acc = acc + big[r_base + tab[ridx_at + 3 * row + k]]
        return acc

    drain1 = reduce_scatter(own_rows, smooth_part, xs, xr, s1, r1, s2, r2, rs_send, rs_recv)

    n = own_rows
    h1 = (n + 1) // 2
    h2 = n - h1

    def make_prolong(t, carry):
        row = col * n + t
        scale = jnp.broadcast_to(weights[row], (128, 128)).T
        ptab[row] = (basis[row].astype(F32) - scale * total[3 * n + t]).astype(BF16)
        return carry

    lax.fori_loop(0, n, make_prolong, 0)

    def spread(y, at, size, sem, dev):
        region = ptab.at[pl.ds((y * 2 + core) * n + at, size)]
        return remote(region, region, ag_send.at[sem], ag_recv.at[sem], dev)

    def arrive(y, c, at, size, sem):
        region = ptab.at[pl.ds((y * 2 + c) * n + at, size)]
        return remote(region, region, ag_send.at[sem], ag_recv.at[sem], dev_x)

    g0 = spread(my, 0, n, 0, dev_a)
    g1 = spread(my, 0, n, 1, dev_b)
    g2 = spread(my, 0, n, 2, dev_x)
    g0.start()
    g1.start()
    g2.start()
    arrive(ya, core, 0, n, 0).wait_recv()
    g3 = spread(ya, 0, h1, 3, dev_b)
    g3.start()
    g5 = spread(ya, 0, n, 5, dev_x)
    g5.start()
    arrive(yb, core, 0, n, 1).wait_recv()
    g4 = spread(yb, h1, h2, 4, dev_a)
    g4.start()
    g6 = spread(yb, 0, n, 6, dev_x)
    g6.start()
    arrive(yo, core, 0, h1, 3).wait_recv()
    g7 = spread(yo, 0, h1, 7, dev_x)
    g7.start()
    arrive(yo, core, h1, h2, 4).wait_recv()
    g8 = spread(yo, h1, h2, 8, dev_x)
    g8.start()

    def drain_halo1(o, carry):
        halo1(o).wait_send()
        return carry

    lax.fori_loop(1, space_count, drain_halo1, 0)
    other = 1 - core
    arrive(my, other, 0, n, 2).wait_recv()
    arrive(ya, other, 0, n, 5).wait_recv()
    arrive(yb, other, 0, n, 6).wait_recv()
    arrive(yo, other, 0, h1, 7).wait_recv()
    arrive(yo, other, h1, h2, 8).wait_recv()

    def send2(o, carry):
        for j in range(CAP):
            stage[o, j] = ptab[asked[o, 0, j]]
        halo2(o).start()
        return carry

    lax.fori_loop(1, space_count, send2, 0)
    drain1()
    for g in (g0, g1, g2, g3, g4, g5, g6, g7, g8):
        g.wait_send()

    def galerkin(slot, tile):
        applied = dot(blocks[slot], tile).astype(BF16)
        return dot_t(ptab[lax.div(slot, 3)], applied)

    group = 4

    def local_galerkin(b, acc):
        parts = []
        for u in range(group):
            code = tab[loc_at + b * group + u]
            parts.append((code >> 15, galerkin(code & 255, ptab[(code >> 8) & 127])))
        for u, (keep, c) in enumerate(parts):
            acc = jnp.where(keep > 0, acc, 0.0) + c
            big[b * group + u] = acc
        return acc

    lax.fori_loop(0, n_local // group, local_galerkin, zero_f)

    def remote_galerkin(o, carry):
        halo2(o).wait_recv()
        for j in range(CAP):
            big[c_base + o * CAP + j] = galerkin(tab[slot_at + o * CAP + j], recv2[o, j])
        return carry

    lax.fori_loop(1, space_count, remote_galerkin, 0)

    def remote_sum(q, acc):
        code = tab[rem_at + q]
        acc = jnp.where((code >> 15) > 0, acc, 0.0) + big[c_base + (code & 127)]
        big[g_base + q] = acc
        return acc

    lax.fori_loop(0, n_remote, remote_sum, zero_f, unroll=4)

    def coarse_part(t):
        return big[tab[last_l_at + t]] + big[tab[last_r_at + t]]

    n_out = NCD * KC // (2 * NY)
    drain2 = reduce_scatter(
        n_out, coarse_part, xs_f, xr_f, s1_f, r1_f, s2_f, r2_f, rf_send, rf_recv
    )
    for t in range(n_out):
        out[t] = total[3 * n_out + t]

    def drain_halo2(o, carry):
        halo2(o).wait_send()
        return carry

    lax.fori_loop(1, space_count, drain_halo2, 0)
    drain2()


def ring_rank(delta, size):
    return jnp.where(delta == 0, 0, jnp.where(2 * delta <= size, 2 * delta - 1, 2 * (size - delta)))


def per_device(
    blocks, basis_tiles, weights, neighbour_device, neighbour_row, counts, aggregate, pair_slot
):
    own = lax.axis_index("space")
    col = lax.axis_index("col")
    space_count = lax.axis_size("space")
    rows, slot_count = neighbour_device.shape
    slots = rows * slot_count
    n_remote = 60
    n_local = slots - n_remote
    peer = neighbour_device.reshape(slots)
    row_of = neighbour_row.reshape(slots)
    remote = peer != own
    live = (
        col * slot_count + jnp.arange(slot_count, dtype=jnp.int32)[None, :] < counts[:, None]
    ).reshape(slots)
    target = (aggregate[:, None] * KC + pair_slot).reshape(slots)
    step = ring_rank((own % NZ - peer % NZ) % NZ, NZ) * NX + ring_rank(
        (own // NZ - peer // NZ) % NX, NX
    )
    ids = jnp.arange(slots, dtype=jnp.int32)
    earlier = ids[None, :] < ids[:, None]
    position = jnp.sum((step[None, :] == step[:, None]) & earlier, axis=1, dtype=jnp.int32)
    bucket = jnp.where(remote, step * CAP + position, 0)
    buckets = jnp.arange(space_count * CAP, dtype=jnp.int32)
    hit = (bucket[None, :] == buckets[:, None]) & remote[None, :]
    packed = jnp.sum(jnp.where(hit, (row_of + 128 * ids)[None, :], 0), axis=1, dtype=jnp.int32)
    lidx = jnp.where(remote | ~live, rows, row_of)
    ridx = jnp.where(live, bucket, 0)
    before = (target[None, :] < target[:, None]) | ((target[None, :] == target[:, None]) & earlier)
    same = (target[None, :] == target[:, None]) & earlier
    kind = remote[None, :] == remote[:, None]
    rank = jnp.sum(before & kind, axis=1, dtype=jnp.int32)
    keep = jnp.any(same & kind, axis=1).astype(jnp.int32)
    code = jnp.where(remote, ridx, ids + 256 * lidx) + (keep << 15)
    place = jnp.where(remote, n_local + rank, rank)
    ordered = jnp.sum(
        jnp.where(place[None, :] == ids[:, None], code[None, :], 0), axis=1, dtype=jnp.int32
    )
    targets = jnp.arange(NCD * KC, dtype=jnp.int32)
    upto = target[None, :] <= targets[:, None]
    equal = target[None, :] == targets[:, None]

    def last(mine, base):
        count = jnp.sum(upto & mine[None, :], axis=1, dtype=jnp.int32)
        some = jnp.any(equal & mine[None, :], axis=1)
        return jnp.where(some, base + count - 1, n_local)

    tab = jnp.concatenate(
        [
            lidx,
            ridx,
            packed >> 7,
            ordered,
            last(~remote, 0),
            last(remote, n_local + space_count * CAP),
        ]
    )
    req = jnp.broadcast_to(
        jnp.pad((packed & 127).reshape(space_count, 1, CAP), ((0, 0), (0, 0), (0, 128 - CAP))),
        (space_count, 8, 128),
    )
    own_rows = rows // (2 * NY)
    n_out = NCD * KC // (2 * NY)
    tile = (128, 128)

    def rs_buffers(n):
        h1 = (n + 1) // 2
        return [
            pltpu.VMEM((4 * n,) + tile, BF16),
            pltpu.VMEM((4 * n,) + tile, BF16),
            pltpu.VMEM((2 * n,) + tile, BF16),
            pltpu.VMEM((2 * n,) + tile, BF16),
            pltpu.VMEM((n,) + tile, BF16),
            pltpu.VMEM((n,) + tile, BF16),
        ]

    dma = pltpu.SemaphoreType.DMA
    return pl.pallas_call(
        functools.partial(kernel, (rows, slots, n_local)),
        out_shape=jax.ShapeDtypeStruct((n_out,) + tile, F32),
        in_specs=[
            pl.BlockSpec(memory_space=pltpu.SMEM),
            pl.BlockSpec(memory_space=pltpu.VMEM),
            pl.BlockSpec(memory_space=pltpu.VMEM),
            pl.BlockSpec(memory_space=pl.ANY),
            pl.BlockSpec(memory_space=pl.ANY),
        ],
        out_specs=pl.BlockSpec(memory_space=pltpu.VMEM),
        scratch_shapes=[
            pltpu.VMEM((slots,) + tile, BF16),
            pltpu.VMEM((rows + 1,) + tile, BF16),
            pltpu.VMEM((rows + 1,) + tile, BF16),
            pltpu.VMEM((space_count, 8, 128), jnp.int32),
            pltpu.SMEM((space_count, 8, 128), jnp.int32),
            pltpu.VMEM((space_count, CAP) + tile, BF16),
            pltpu.VMEM((space_count, CAP) + tile, BF16),
            pltpu.VMEM((space_count, CAP) + tile, BF16),
            pltpu.VMEM((n_local + space_count * CAP + n_remote,) + tile, F32),
            pltpu.VMEM((4 * own_rows,) + tile, F32),
            *rs_buffers(own_rows),
            *rs_buffers(n_out),
            dma((3,)),
            *([dma((space_count,))] * 6),
            *([dma((10,))] * 4),
            *([dma((9,))] * 2),
        ],
        compiler_params=pltpu.CompilerParams(
            collective_id=0, has_side_effects=True, vmem_limit_bytes=62 << 20
        ),
        name="galerkin_step",
    )(
        tab,
        req,
        weights.reshape(rows, 1, 128),
        blocks.reshape((slots,) + tile),
        basis_tiles,
    )


def solution(mesh):
    return jax.shard_map(
        per_device,
        mesh=mesh,
        in_specs=(
            P("space", "col", None, None),
            P("space", None, None),
            P("space", None),
            P("space", "col"),
            P("space", "col"),
            P("space"),
            P("space"),
            P("space", "col"),
        ),
        out_specs=P(("space", "col"), None, None),
        check_vma=False,
    )
```

```python
import functools

import jax
import jax.numpy as jnp
from jax import lax
from jax.experimental import pallas as pl
from jax.experimental.pallas import tpu as pltpu
from jax.sharding import PartitionSpec as P

KC = 4
CAP = 3
NCD = 10
NX, NZ, NY = 4, 8, 4
MESH = pl.DeviceIdType.MESH
F32 = jnp.float32
BF16 = jnp.bfloat16
HALF = 64
S_WIRE = BF16
C_WIRE = BF16


def dot_nt(a, b):
    return lax.dot_general(a, b, (((1,), (1,)), ((), ())), preferred_element_type=F32)


def step_offset(o):
    zi, xi = o // NX, o % NX
    hz, hx = (zi + 1) // 2, (xi + 1) // 2
    dz = ((zi % 2) * hz + (1 - zi % 2) * (NZ - hz)) % NZ
    dx = ((xi % 2) * hx + (1 - xi % 2) * (NX - hx)) % NX
    return dx, dz


def kernel(
    sizes,
    fields,
    weights,
    blocks_hbm,
    basis_hbm,
    out,
    blocks,
    basis,
    table,
    ptab,
    req,
    tab_v,
    tab,
    asked_v,
    asked,
    stage,
    recv1,
    recv2,
    big,
    total,
    coarse_t,
    xs,
    xr,
    s1,
    r1,
    s2,
    r2,
    xs_f,
    xr_f,
    s1_f,
    r1_f,
    s2_f,
    r2_f,
    load_sem,
    req_send,
    req_recv,
    a_send,
    a_recv,
    b_send,
    b_recv,
    rs_send,
    rs_recv,
    rf_send,
    rf_recv,
    ag_send,
    ag_recv,
):
    rows, slots, n_local = sizes
    space_count = NX * NZ
    peers = space_count - 1
    own_rows = rows // (2 * NY)
    n_remote = slots - n_local
    r_base = rows
    c_base = n_local
    g_base = n_local + space_count * CAP

    me = lax.axis_index("space")
    col = lax.axis_index("col")
    mx, mz = me // NZ, me % NZ
    my, core = col // 2, col % 2
    ya = my + 1 - 2 * (my % 2)
    yb = NY - 1 - my
    yo = (my + 2) % NY
    dev_x = (me, my * 2 + 1 - core)
    dev_a = (me, ya * 2 + core)
    dev_b = (me, yb * 2 + core)

    def target(o):
        dx, dz = step_offset(o)
        return (((mx + dx) % NX) * NZ + (mz + dz) % NZ, col)

    def origin(o):
        dx, dz = step_offset(o)
        return (((mx + NX - dx) % NX) * NZ + (mz + NZ - dz) % NZ, col)

    load_a = pltpu.make_async_copy(blocks_hbm, blocks, load_sem.at[0])
    load_b = pltpu.make_async_copy(basis_hbm, basis, load_sem.at[1])
    load_b.start()
    load_a.start()

    barrier = pltpu.get_barrier_semaphore()

    def greet(o, carry):
        pl.semaphore_signal(barrier, 1, device_id=target(o), device_id_type=MESH)
        return carry

    lax.fori_loop(1, space_count, greet, 0)
    for peer in (dev_x, dev_a, dev_b):
        pl.semaphore_signal(barrier, 1, device_id=peer, device_id_type=MESH)
    zero_b = jnp.zeros((2, HALF, 128), BF16)
    zero_f = jnp.zeros((2, HALF, 128), F32)
    table[rows] = zero_b
    ptab[0, rows] = zero_b[0]
    ptab[1, rows] = zero_b[0]
    big[r_base] = zero_f
    big[c_base] = zero_f

    cols = fields[...]
    lines = cols.T

    def col_of(m, k):
        return m[:, k : k + 1]

    def line_of(m, k):
        return m[k : k + 1, :]

    def fold(m):
        return jnp.sum(m.astype(jnp.int32), axis=0, keepdims=True)

    sub = lax.broadcasted_iota(jnp.int32, (128, 128), 0)
    lane = lax.broadcasted_iota(jnp.int32, (128, 128), 1)
    lane_row = lax.broadcasted_iota(jnp.int32, (1, 128), 1)
    sub_col = lax.broadcasted_iota(jnp.int32, (128, 1), 0)
    prior = sub < lane
    blank = jnp.zeros((1, 128), jnp.int32)

    def ahead(same, less, k, k2):
        if k2 < k:
            return same | less
        if k2 > k:
            return less
        return (same & prior) | less

    none = jnp.zeros((128, 128), jnp.bool_)
    bucket_line = []
    for k in range(3):
        step = line_of(lines, k)
        position = blank
        for k2 in range(3):
            same = col_of(cols, k2) == step
            position = position + fold(ahead(same, none, k, k2))
        bucket_line.append(jnp.where(step > 0, step * CAP + position, 0))

    def upright(rows_):
        return jnp.concatenate(
            rows_ + [jnp.zeros((128 - len(rows_), 128), jnp.int32)], axis=0
        ).T

    bucket = upright(bucket_line)
    packed = blank
    for k in range(3):
        match = (col_of(bucket, k) == lane) & (col_of(cols, k) > 0)
        packed = packed + fold(
            jnp.where(match, col_of(cols, 3 + k) + 128 * (3 * sub_col + k), 0)
        )
    req[0] = packed & 127
    pl.semaphore_wait(barrier, peers + 3)

    def remote(src, dst, send, recv, dev):
        return pltpu.make_async_remote_copy(
            src, dst, send, recv, device_id=dev, device_id_type=MESH
        )

    def ask(o):
        return remote(req, asked_v.at[o], req_send.at[o], req_recv.at[o], origin(o))

    def ask_start(o, carry):
        ask(o).start()
        return carry

    lax.fori_loop(1, space_count, ask_start, 0)
    live = [line_of(lines, 9 + k) for k in range(3)]
    for k in range(3):
        local_tile = jnp.where(
            (line_of(lines, k) == 0) & (live[k] > 0), line_of(lines, 3 + k), rows
        )
        tab_v[k : k + 1, :] = local_tile
        tab_v[3 + k : 4 + k, :] = jnp.where(live[k] > 0, bucket_line[k], 0)
    tab_v[6:7, :] = packed >> 7
    code_line, place_line = [], []
    for k in range(3):
        step = line_of(lines, k)
        goal = line_of(lines, 6 + k)
        rank, again = blank, blank
        for k2 in range(3):
            kind = (
                ((col_of(cols, k2) > 0) & (step > 0)) | ((col_of(cols, k2) == 0) & (step == 0))
            )
            same = (col_of(cols, 6 + k2) == goal) & kind
            less = (col_of(cols, 6 + k2) < goal) & kind
            rank = rank + fold(ahead(same, less, k, k2))
            again = again + fold(ahead(same, none, k, k2))
        keep_bit = jnp.where(again > 0, 1 << 15, 0)
        code_line.append(
            keep_bit
            + jnp.where(
                step > 0,
                tab_v[3 + k : 4 + k, :],
                jnp.minimum(3 * lane_row + k, slots - 1) + 256 * tab_v[k : k + 1, :],
            )
        )
        place_line.append(
            jnp.where(step > 0, 256 + rank, jnp.where(step == 0, rank, 1024))
        )
    sorted_cols = upright(code_line + place_line)
    for part in range(3):
        listed = blank
        for k in range(3):
            listed = listed + fold(
                jnp.where(
                    col_of(sorted_cols, 3 + k) == lane + 128 * part, col_of(sorted_cols, k), 0
                )
            )
        tab_v[7 + part : 8 + part, :] = listed
    for kind_at, first, size in ((10, 0, n_local), (11, g_base, n_remote)):
        count, some = blank, blank
        for k in range(3):
            mine = (col_of(cols, k) > 0) if first else (col_of(cols, k) == 0)
            goal = col_of(cols, 6 + k)
            count = count + fold((goal <= lane) & mine)
            some = some + fold((goal == lane) & mine)
        tab_v[kind_at : kind_at + 1, :] = jnp.where(
            some > 0, first + jnp.minimum(count, size) - 1, c_base
        )
    tab_copy = pltpu.make_async_copy(tab_v, tab, load_sem.at[3])
    tab_copy.start()
    load_b.wait()

    def flip(i, carry):
        table[i] = basis[i].T.reshape(2, HALF, 128)
        return carry

    lax.fori_loop(0, rows, flip, 0, unroll=2)

    def ask_wait(o, carry):
        ask(o).wait()
        return carry

    lax.fori_loop(1, space_count, ask_wait, 0)
    to_scalar = pltpu.make_async_copy(
        asked_v.at[pl.ds(1, peers)], asked.at[pl.ds(1, peers)], load_sem.at[2]
    )
    to_scalar.start()
    to_scalar.wait()
    tab_copy.wait()

    def held(value, last):
        return jnp.minimum(jnp.maximum(value, 0), last)

    def halo(recv, send_sem, recv_sem, h, o):
        return remote(
            stage.at[h, o],
            recv.at[h, o],
            send_sem.at[h * space_count + o],
            recv_sem.at[h * space_count + o],
            target(o),
        )

    halo1 = functools.partial(halo, recv1, a_send, a_recv)
    halo2 = functools.partial(halo, recv2, b_send, b_recv)

    def each_peer(body):
        def step(o, carry):
            body(o)
            return carry

        lax.fori_loop(1, space_count, step, 0)

    def send1(h):
        def one(o):
            for j in range(CAP):
                stage[h, o, j] = table[held(asked[o, 0, 0, o * CAP + j], rows), h]
            halo1(h, o).start()

        each_peer(one)

    send1(0)
    load_a.wait()

    def local_smooth(i, carry):
        lhs = jnp.concatenate(
            [table[held(tab[k, i], rows)].reshape(128, 128) for k in range(3)], axis=1
        )
        rhs = jnp.concatenate([blocks[3 * i + k] for k in range(3)], axis=1)
        big[i] = dot_nt(lhs, rhs).reshape(2, HALF, 128)
        return carry

    lax.fori_loop(0, rows, local_smooth, 0, unroll=2)
    send1(1)

    def remote_smooth(h):
        def one(o):
            halo1(h, o).wait_recv()
            for j in range(CAP):
                big[r_base + o * CAP + j, h] = dot_nt(
                    recv1[h, o, j], blocks[held(tab[6, o * CAP + j], slots - 1)]
                )

        each_peer(one)

    def reduce_scatter(n, part, xs, xr, s1, r1, s2, r2, send, recv, base):
        groups = (ya, yb, yo, my)
        h1 = (n + 1) // 2
        h2 = n - h1
        kind = xs.dtype

        def swap(i):
            return remote(
                xs.at[pl.ds(i * n, n)],
                xr.at[pl.ds(i * n, n)],
                send.at[base + i],
                recv.at[base + i],
                dev_x,
            )

        for i in range(4):

            def fill(t, carry):
                xs[i * n + t] = part((groups[i] * 2 + 1 - core) * n + t).astype(kind)
                return carry

            lax.fori_loop(0, n, fill, 0, unroll=n)
            swap(i).start()
        for i in range(4):

            def keep(t, carry):
                total[i * n + t] = part((groups[i] * 2 + core) * n + t)
                return carry

            lax.fori_loop(0, n, keep, 0, unroll=n)

        def hop(src, dst, at, size, sem, dev):
            return remote(
                src.at[pl.ds(at, size)],
                dst.at[pl.ds(at, size)],
                send.at[base + sem],
                recv.at[base + sem],
                dev,
            )

        m0 = hop(s1, r1, 0, h1, 4, dev_a)
        m1 = hop(s1, r1, h1, h1, 5, dev_a)
        m2 = hop(s1, r1, 2 * h1, h2, 6, dev_b)
        m3 = hop(s1, r1, 2 * h1 + h2, h2, 7, dev_b)
        m4 = hop(s2, r2, 0, h1, 8, dev_b)
        m5 = hop(s2, r2, h1, h2, 9, dev_a)

        def add_swapped(i):
            swap(i).wait_recv()
            for t in range(n):
                total[i * n + t] += xr[i * n + t].astype(F32)

        def put(dst, at, first, size):
            for t in range(size):
                dst[at + t] = total[first + t].astype(kind)

        def take(src, at, first, size):
            for t in range(size):
                total[first + t] += src[at + t].astype(F32)

        add_swapped(0)
        put(s1, 0, 0, h1)
        m0.start()
        add_swapped(1)
        put(s1, 2 * h1, n + h1, h2)
        m2.start()
        add_swapped(2)
        put(s1, h1, 2 * n, h1)
        m1.start()
        put(s1, 2 * h1 + h2, 2 * n + h1, h2)
        m3.start()
        add_swapped(3)
        m1.wait_recv()
        take(r1, h1, n, h1)
        put(s2, 0, n, h1)
        m4.start()
        m3.wait_recv()
        take(r1, 2 * h1 + h2, h1, h2)
        put(s2, h1, h1, h2)
        m5.start()
        m0.wait_recv()
        take(r1, 0, 3 * n, h1)
        m2.wait_recv()
        take(r1, 2 * h1, 3 * n + h1, h2)
        m4.wait_recv()
        take(r2, 0, 3 * n, h1)
        m5.wait_recv()
        take(r2, h1, 3 * n + h1, h2)

        def drain():
            for i in range(4):
                swap(i).wait_send()
            for m in (m0, m1, m2, m3, m4, m5):
                m.wait_send()

        return drain

    n = own_rows
    n1 = (n + 1) // 2
    n2 = n - n1
    other = 1 - core

    def make_prolong(h):
        def smooth_part(row):
            acc = big[row, h]
            for k in range(3):
                acc = acc + big[r_base + held(tab[3 + k, row], space_count * CAP - 1), h]
            return acc

        reduce_scatter(
            n, smooth_part, xs, xr, s1, r1, s2, r2, rs_send, rs_recv, 10 * h
        )()
        for t in range(n):
            row = col * n + t
            ptab[h, row] = (table[row, h].astype(F32) - weights[row] * total[3 * n + t]).astype(
                BF16
            )

        def spread(y, at, size, sem, dev):
            region = ptab.at[h, pl.ds((y * 2 + core) * n + at, size)]
            return remote(region, region, ag_send.at[9 * h + sem], ag_recv.at[9 * h + sem], dev)

        def arrive(y, c, at, size, sem):
            region = ptab.at[h, pl.ds((y * 2 + c) * n + at, size)]
            remote(
                region, region, ag_send.at[9 * h + sem], ag_recv.at[9 * h + sem], dev_x
            ).wait_recv()

        sent = []

        def go(*args):
            copy = spread(*args)
            copy.start()
            sent.append(copy)

        go(my, 0, n, 0, dev_a)
        go(my, 0, n, 1, dev_b)
        go(my, 0, n, 2, dev_x)
        arrive(ya, core, 0, n, 0)
        go(ya, 0, n1, 3, dev_b)
        go(ya, 0, n, 5, dev_x)
        arrive(yb, core, 0, n, 1)
        go(yb, n1, n2, 4, dev_a)
        go(yb, 0, n, 6, dev_x)
        arrive(yo, core, 0, n1, 3)
        go(yo, 0, n1, 7, dev_x)
        arrive(yo, core, n1, n2, 4)
        go(yo, n1, n2, 8, dev_x)
        arrive(my, other, 0, n, 2)
        arrive(ya, other, 0, n, 5)
        arrive(yb, other, 0, n, 6)
        arrive(yo, other, 0, n1, 7)
        arrive(yo, other, n1, n2, 8)
        return sent

    def send2(h):
        def one(o):
            halo1(h, o).wait_send()
            for j in range(CAP):
                stage[h, o, j] = ptab[h, held(asked[o, 0, 0, o * CAP + j], rows)]
            halo2(h, o).start()

        each_peer(one)

    for h in range(2):
        remote_smooth(h)
        sent = make_prolong(h)
        send2(h)
        for copy in sent:
            copy.wait_send()

    def whole(row):
        return jnp.concatenate([ptab[0, row], ptab[1, row]], axis=0)

    def galerkin(slot, tile):
        applied = dot_nt(tile, blocks[slot]).astype(BF16)
        return dot_nt(applied, whole(lax.div(slot, 3)))

    group = 4

    def local_galerkin(b, acc):
        parts = []
        for u in range(group):
            q = b * group + u
            code = tab[7 + q // 128, q % 128]
            parts.append((code >> 15, galerkin(held(code & 255, slots - 1), whole(held((code >> 8) & 127, rows)))))
        for u, (keep, c) in enumerate(parts):
            acc = jnp.where(keep > 0, acc, 0.0) + c
            big[b * group + u] = acc.reshape(2, HALF, 128)
        return acc

    lax.fori_loop(0, n_local // group, local_galerkin, jnp.zeros((128, 128), F32))

    n_out = NCD * KC // (2 * NY)

    def finish(h):
        def one(o):
            halo2(h, o).wait_recv()
            for j in range(CAP):
                big[c_base + o * CAP + j, h] = galerkin(
                    held(tab[6, o * CAP + j], slots - 1), recv2[h, o, j]
                )

        each_peer(one)

        def remote_sum(q, acc):
            code = tab[9, q]
            acc = jnp.where((code >> 15) > 0, acc, 0.0) + big[c_base + held(code & 127, space_count * CAP - 1), h]
            big[g_base + q, h] = acc
            return acc

        lax.fori_loop(0, n_remote, remote_sum, jnp.zeros((HALF, 128), F32), unroll=4)

        def coarse_part(t):
            end = big.shape[0] - 1
            return big[held(tab[10, t], end), h] + big[held(tab[11, t], end), h]

        bufs = [b.at[h] for b in (xs_f, xr_f, s1_f, r1_f, s2_f, r2_f)]
        drain = reduce_scatter(n_out, coarse_part, *bufs, rf_send, rf_recv, 10 * h)
        for t in range(n_out):
            coarse_t[t, h] = total[3 * n_out + t]
        return drain

    drains = [finish(h) for h in range(2)]
    for t in range(n_out):
        out[t] = coarse_t[t].reshape(128, 128).T
    for h in range(2):
        each_peer(lambda o: halo2(h, o).wait_send())
        drains[h]()


def ring_rank(delta, size):
    return jnp.where(delta == 0, 0, jnp.where(2 * delta <= size, 2 * delta - 1, 2 * (size - delta)))


def per_device(
    blocks, basis_tiles, weights, neighbour_device, neighbour_row, counts, aggregate, pair_slot
):
    own = lax.axis_index("space")
    col = lax.axis_index("col")
    space_count = lax.axis_size("space")
    rows, slot_count = neighbour_device.shape
    slots = rows * slot_count
    n_remote = 60
    n_local = slots - n_remote
    live = (
        col * slot_count + jnp.arange(slot_count, dtype=jnp.int32)[None, :] < counts[:, None]
    )
    target = aggregate[:, None] * KC + pair_slot
    step = ring_rank((own % NZ - neighbour_device % NZ) % NZ, NZ) * NX + ring_rank(
        (own // NZ - neighbour_device // NZ) % NX, NX
    )
    fields = jnp.concatenate(
        [step, neighbour_row, target, live.astype(jnp.int32)], axis=1
    )
    fields = jnp.pad(
        fields, ((0, 128 - rows), (0, 128 - 4 * slot_count)), constant_values=-1
    )
    own_rows = rows // (2 * NY)
    n_out = NCD * KC // (2 * NY)
    tile = (128, 128)
    half = (HALF, 128)

    def rs_buffers(lead, n, kind):
        return [pltpu.VMEM(lead + (m * n,) + half, kind) for m in (4, 4, 2, 2, 1, 1)]

    dma = pltpu.SemaphoreType.DMA
    return pl.pallas_call(
        functools.partial(kernel, (rows, slots, n_local)),
        out_shape=jax.ShapeDtypeStruct((n_out,) + tile, F32),
        in_specs=[
            pl.BlockSpec(memory_space=pltpu.VMEM),
            pl.BlockSpec(memory_space=pltpu.VMEM),
            pl.BlockSpec(memory_space=pl.ANY),
            pl.BlockSpec(memory_space=pl.ANY),
        ],
        out_specs=pl.BlockSpec(memory_space=pltpu.VMEM),
        scratch_shapes=[
            pltpu.VMEM((slots,) + tile, BF16),
            pltpu.VMEM((rows,) + tile, BF16),
            pltpu.VMEM((rows + 1, 2) + half, BF16),
            pltpu.VMEM((2, rows + 1) + half, BF16),
            pltpu.VMEM((1, 1, 128), jnp.int32),
            pltpu.VMEM((16, 128), jnp.int32),
            pltpu.SMEM((16, 128), jnp.int32),
            pltpu.VMEM((space_count, 1, 1, 128), jnp.int32),
            pltpu.SMEM((space_count, 1, 1, 128), jnp.int32),
            pltpu.VMEM((2, space_count, CAP) + half, BF16),
            pltpu.VMEM((2, space_count, CAP) + half, BF16),
            pltpu.VMEM((2, space_count, CAP) + half, BF16),
            pltpu.VMEM((n_local + space_count * CAP + n_remote, 2) + half, F32),
            pltpu.VMEM((4 * own_rows,) + half, F32),
            pltpu.VMEM((n_out, 2) + half, F32),
            *rs_buffers((), own_rows, S_WIRE),
            *rs_buffers((2,), n_out, C_WIRE),
            dma((4,)),
            *([dma((space_count,))] * 2),
            *([dma((2 * space_count,))] * 4),
            *([dma((20,))] * 4),
            *([dma((18,))] * 2),
        ],
        compiler_params=pltpu.CompilerParams(
            collective_id=0, has_side_effects=True, vmem_limit_bytes=62 << 20
        ),
        name="galerkin_step",
    )(
        fields,
        weights.reshape(rows, 1, 128),
        blocks.reshape((slots,) + tile),
        basis_tiles,
    )


def solution(mesh):
    return jax.shard_map(
        per_device,
        mesh=mesh,
        in_specs=(
            P("space", "col", None, None),
            P("space", None, None),
            P("space", None),
            P("space", "col"),
            P("space", "col"),
            P("space"),
            P("space"),
            P("space", "col"),
        ),
        out_specs=P(("space", "col"), None, None),
        check_vma=False,
    )
```

```python
import functools

import jax
import jax.numpy as jnp
from jax import lax
from jax.experimental import pallas as pl
from jax.experimental.pallas import tpu as pltpu
from jax.sharding import PartitionSpec as P

KC = 4
CAP = 3
NCD = 10
NX, NZ, NY = 4, 8, 4
MESH = pl.DeviceIdType.MESH
F32 = jnp.float32
BF16 = jnp.bfloat16
HALF = 64
S_WIRE = BF16
C_WIRE = BF16


def dot_nt(a, b):
    return lax.dot_general(a, b, (((1,), (1,)), ((), ())), preferred_element_type=F32)


def step_offset(o):
    zi, xi = o // NX, o % NX
    hz, hx = (zi + 1) // 2, (xi + 1) // 2
    dz = ((zi % 2) * hz + (1 - zi % 2) * (NZ - hz)) % NZ
    dx = ((xi % 2) * hx + (1 - xi % 2) * (NX - hx)) % NX
    return dx, dz


def kernel(
    sizes,
    fields,
    weights,
    blocks_hbm,
    basis_hbm,
    out,
    blocks,
    basis,
    table,
    ptab,
    req,
    tab_v,
    tab,
    asked_v,
    asked,
    stage,
    recv1,
    recv2,
    big,
    total,
    xs,
    xr,
    s1,
    r1,
    s2,
    r2,
    xs_f,
    xr_f,
    s1_f,
    r1_f,
    s2_f,
    r2_f,
    load_sem,
    req_send,
    req_recv,
    a_send,
    a_recv,
    b_send,
    b_recv,
    rs_send,
    rs_recv,
    rf_send,
    rf_recv,
    ag_send,
    ag_recv,
):
    rows, slots, n_local = sizes
    space_count = NX * NZ
    peers = space_count - 1
    own_rows = rows // (2 * NY)
    n_remote = slots - n_local
    r_base = rows
    c_base = n_local
    g_base = n_local + space_count * CAP

    me = lax.axis_index("space")
    col = lax.axis_index("col")
    mx, mz = me // NZ, me % NZ
    my, core = col // 2, col % 2
    ya = my + 1 - 2 * (my % 2)
    yb = NY - 1 - my
    yo = (my + 2) % NY
    dev_x = (me, my * 2 + 1 - core)
    dev_a = (me, ya * 2 + core)
    dev_b = (me, yb * 2 + core)

    def target(o):
        dx, dz = step_offset(o)
        return (((mx + dx) % NX) * NZ + (mz + dz) % NZ, col)

    def origin(o):
        dx, dz = step_offset(o)
        return (((mx + NX - dx) % NX) * NZ + (mz + NZ - dz) % NZ, col)

    load_a = pltpu.make_async_copy(blocks_hbm, blocks, load_sem.at[0])
    load_b = pltpu.make_async_copy(basis_hbm, basis, load_sem.at[1])
    load_b.start()
    load_a.start()

    barrier = pltpu.get_barrier_semaphore()

    def greet(o, carry):
        pl.semaphore_signal(barrier, 1, device_id=target(o), device_id_type=MESH)
        return carry

    lax.fori_loop(1, space_count, greet, 0)
    for peer in (dev_x, dev_a, dev_b):
        pl.semaphore_signal(barrier, 1, device_id=peer, device_id_type=MESH)
    zero_b = jnp.zeros((2, HALF, 128), BF16)
    zero_f = jnp.zeros((2, HALF, 128), F32)
    table[rows] = zero_b
    ptab[0, rows] = zero_b[0]
    ptab[1, rows] = zero_b[0]
    big[r_base] = zero_f
    big[c_base] = zero_f

    cols = fields[...]
    lines = cols.T

    def col_of(m, k):
        return m[:, k : k + 1]

    def line_of(m, k):
        return m[k : k + 1, :]

    def fold(m):
        return jnp.sum(m.astype(jnp.int32), axis=0, keepdims=True)

    sub = lax.broadcasted_iota(jnp.int32, (128, 128), 0)
    lane = lax.broadcasted_iota(jnp.int32, (128, 128), 1)
    lane_row = lax.broadcasted_iota(jnp.int32, (1, 128), 1)
    sub_col = lax.broadcasted_iota(jnp.int32, (128, 1), 0)
    prior = sub < lane
    blank = jnp.zeros((1, 128), jnp.int32)

    def ahead(same, less, k, k2):
        if k2 < k:
            return same | less
        if k2 > k:
            return less
        return (same & prior) | less

    none = jnp.zeros((128, 128), jnp.bool_)
    bucket_line = []
    for k in range(3):
        step = line_of(lines, k)
        position = blank
        for k2 in range(3):
            same = col_of(cols, k2) == step
            position = position + fold(ahead(same, none, k, k2))
        bucket_line.append(jnp.where(step > 0, step * CAP + position, 0))

    def upright(rows_):
        return jnp.concatenate(
            rows_ + [jnp.zeros((128 - len(rows_), 128), jnp.int32)], axis=0
        ).T

    bucket = upright(bucket_line)
    packed = blank
    for k in range(3):
        match = (col_of(bucket, k) == lane) & (col_of(cols, k) > 0)
        packed = packed + fold(
            jnp.where(match, col_of(cols, 3 + k) + 128 * (3 * sub_col + k), 0)
        )
    req[0] = packed & 127
    pl.semaphore_wait(barrier, peers + 3)

    def remote(src, dst, send, recv, dev):
        return pltpu.make_async_remote_copy(
            src, dst, send, recv, device_id=dev, device_id_type=MESH
        )

    def ask(o):
        return remote(req, asked_v.at[o], req_send.at[o], req_recv.at[o], origin(o))

    def ask_start(o, carry):
        ask(o).start()
        return carry

    lax.fori_loop(1, space_count, ask_start, 0)
    live = [line_of(lines, 9 + k) for k in range(3)]
    for k in range(3):
        local_tile = jnp.where(
            (line_of(lines, k) == 0) & (live[k] > 0), line_of(lines, 3 + k), rows
        )
        tab_v[k : k + 1, :] = local_tile
        tab_v[3 + k : 4 + k, :] = jnp.where(live[k] > 0, bucket_line[k], 0)
    tab_v[6:7, :] = packed >> 7
    code_line, place_line = [], []
    for k in range(3):
        step = line_of(lines, k)
        goal = line_of(lines, 6 + k)
        rank, again = blank, blank
        for k2 in range(3):
            kind = (
                ((col_of(cols, k2) > 0) & (step > 0)) | ((col_of(cols, k2) == 0) & (step == 0))
            )
            same = (col_of(cols, 6 + k2) == goal) & kind
            less = (col_of(cols, 6 + k2) < goal) & kind
            rank = rank + fold(ahead(same, less, k, k2))
            again = again + fold(ahead(same, none, k, k2))
        keep_bit = jnp.where(again > 0, 1 << 15, 0)
        code_line.append(
            keep_bit
            + jnp.where(
                step > 0,
                tab_v[3 + k : 4 + k, :],
                jnp.minimum(3 * lane_row + k, slots - 1) + 256 * tab_v[k : k + 1, :],
            )
        )
        place_line.append(
            jnp.where(step > 0, 256 + rank, jnp.where(step == 0, rank, 1024))
        )
    sorted_cols = upright(code_line + place_line)
    for part in range(3):
        listed = blank
        for k in range(3):
            listed = listed + fold(
                jnp.where(
                    col_of(sorted_cols, 3 + k) == lane + 128 * part, col_of(sorted_cols, k), 0
                )
            )
        tab_v[7 + part : 8 + part, :] = listed
    for kind_at, first, size in ((10, 0, n_local), (11, g_base, n_remote)):
        count, some = blank, blank
        for k in range(3):
            mine = (col_of(cols, k) > 0) if first else (col_of(cols, k) == 0)
            goal = col_of(cols, 6 + k)
            count = count + fold((goal <= lane) & mine)
            some = some + fold((goal == lane) & mine)
        tab_v[kind_at : kind_at + 1, :] = jnp.where(
            some > 0, first + jnp.minimum(count, size) - 1, c_base
        )
    tab_copy = pltpu.make_async_copy(tab_v, tab, load_sem.at[3])
    tab_copy.start()
    load_b.wait()

    def flip(i, carry):
        table[i] = basis[i].T.reshape(2, HALF, 128)
        return carry

    lax.fori_loop(0, rows, flip, 0, unroll=2)

    def ask_wait(o, carry):
        ask(o).wait()
        return carry

    lax.fori_loop(1, space_count, ask_wait, 0)
    to_scalar = pltpu.make_async_copy(
        asked_v.at[pl.ds(1, peers)], asked.at[pl.ds(1, peers)], load_sem.at[2]
    )
    to_scalar.start()
    to_scalar.wait()
    tab_copy.wait()

    def held(value, last):
        return jnp.minimum(jnp.maximum(value, 0), last)

    def halo(recv, send_sem, recv_sem, h, o):
        return remote(
            stage.at[h, o],
            recv.at[h, o],
            send_sem.at[h * space_count + o],
            recv_sem.at[h * space_count + o],
            target(o),
        )

    halo1 = functools.partial(halo, recv1, a_send, a_recv)
    halo2 = functools.partial(halo, recv2, b_send, b_recv)

    def each_peer(body):
        def step(o, carry):
            body(o)
            return carry

        lax.fori_loop(1, space_count, step, 0)

    def send1(h):
        def one(o):
            for j in range(CAP):
                stage[h, o, j] = table[held(asked[o, 0, 0, o * CAP + j], rows), h]
            halo1(h, o).start()

        each_peer(one)

    send1(0)
    load_a.wait()

    def local_smooth(i, carry):
        lhs = jnp.concatenate(
            [table[held(tab[k, i], rows)].reshape(128, 128) for k in range(3)], axis=1
        )
        rhs = jnp.concatenate([blocks[3 * i + k] for k in range(3)], axis=1)
        big[i] = dot_nt(lhs, rhs).reshape(2, HALF, 128)
        return carry

    lax.fori_loop(0, rows, local_smooth, 0, unroll=2)
    send1(1)

    def remote_smooth(h):
        def one(o):
            halo1(h, o).wait_recv()
            for j in range(CAP):
                big[r_base + o * CAP + j, h] = dot_nt(
                    recv1[h, o, j], blocks[held(tab[6, o * CAP + j], slots - 1)]
                )

        each_peer(one)

    def reduce_scatter(n, part, xs, xr, s1, r1, s2, r2, send, recv, base):
        groups = (ya, yb, yo, my)
        h1 = (n + 1) // 2
        h2 = n - h1
        kind = xs.dtype

        def swap(i):
            return remote(
                xs.at[pl.ds(i * n, n)],
                xr.at[pl.ds(i * n, n)],
                send.at[base + i],
                recv.at[base + i],
                dev_x,
            )

        for i in range(4):

            def fill(t, carry):
                xs[i * n + t] = part((groups[i] * 2 + 1 - core) * n + t).astype(kind)
                return carry

            lax.fori_loop(0, n, fill, 0, unroll=n)
            swap(i).start()
        for i in range(4):

            def keep(t, carry):
                total[i * n + t] = part((groups[i] * 2 + core) * n + t)
                return carry

            lax.fori_loop(0, n, keep, 0, unroll=n)

        def hop(src, dst, at, size, sem, dev):
            return remote(
                src.at[pl.ds(at, size)],
                dst.at[pl.ds(at, size)],
                send.at[base + sem],
                recv.at[base + sem],
                dev,
            )

        m0 = hop(s1, r1, 0, h1, 4, dev_a)
        m1 = hop(s1, r1, h1, h1, 5, dev_a)
        m2 = hop(s1, r1, 2 * h1, h2, 6, dev_b)
        m3 = hop(s1, r1, 2 * h1 + h2, h2, 7, dev_b)
        m4 = hop(s2, r2, 0, h1, 8, dev_b)
        m5 = hop(s2, r2, h1, h2, 9, dev_a)

        def add_swapped(i):
            swap(i).wait_recv()
            for t in range(n):
                total[i * n + t] += xr[i * n + t].astype(F32)

        def put(dst, at, first, size):
            for t in range(size):
                dst[at + t] = total[first + t].astype(kind)

        def take(src, at, first, size):
            for t in range(size):
                total[first + t] += src[at + t].astype(F32)

        add_swapped(0)
        put(s1, 0, 0, h1)
        m0.start()
        add_swapped(1)
        put(s1, 2 * h1, n + h1, h2)
        m2.start()
        add_swapped(2)
        put(s1, h1, 2 * n, h1)
        m1.start()
        put(s1, 2 * h1 + h2, 2 * n + h1, h2)
        m3.start()
        add_swapped(3)
        m1.wait_recv()
        take(r1, h1, n, h1)
        put(s2, 0, n, h1)
        m4.start()
        m3.wait_recv()
        take(r1, 2 * h1 + h2, h1, h2)
        put(s2, h1, h1, h2)
        m5.start()
        m0.wait_recv()
        take(r1, 0, 3 * n, h1)
        m2.wait_recv()
        take(r1, 2 * h1, 3 * n + h1, h2)
        m4.wait_recv()
        take(r2, 0, 3 * n, h1)
        m5.wait_recv()
        take(r2, h1, 3 * n + h1, h2)

        def drain():
            for i in range(4):
                swap(i).wait_send()
            for m in (m0, m1, m2, m3, m4, m5):
                m.wait_send()

        return drain

    n = own_rows
    n1 = (n + 1) // 2
    n2 = n - n1
    other = 1 - core

    def make_prolong(h):
        def smooth_part(row):
            acc = big[row, h]
            for k in range(3):
                acc = acc + big[r_base + held(tab[3 + k, row], space_count * CAP - 1), h]
            return acc

        reduce_scatter(
            n, smooth_part, xs, xr, s1, r1, s2, r2, rs_send, rs_recv, 10 * h
        )()
        for t in range(n):
            row = col * n + t
            ptab[h, row] = (table[row, h].astype(F32) - weights[row] * total[3 * n + t]).astype(
                BF16
            )

        def spread(y, at, size, sem, dev):
            region = ptab.at[h, pl.ds((y * 2 + core) * n + at, size)]
            return remote(region, region, ag_send.at[9 * h + sem], ag_recv.at[9 * h + sem], dev)

        def arrive(y, c, at, size, sem):
            region = ptab.at[h, pl.ds((y * 2 + c) * n + at, size)]
            remote(
                region, region, ag_send.at[9 * h + sem], ag_recv.at[9 * h + sem], dev_x
            ).wait_recv()

        sent = []

        def go(*args):
            copy = spread(*args)
            copy.start()
            sent.append(copy)

        go(my, 0, n, 0, dev_a)
        go(my, 0, n, 1, dev_b)
        go(my, 0, n, 2, dev_x)
        arrive(ya, core, 0, n, 0)
        go(ya, 0, n1, 3, dev_b)
        go(ya, 0, n, 5, dev_x)
        arrive(yb, core, 0, n, 1)
        go(yb, n1, n2, 4, dev_a)
        go(yb, 0, n, 6, dev_x)
        arrive(yo, core, 0, n1, 3)
        go(yo, 0, n1, 7, dev_x)
        arrive(yo, core, n1, n2, 4)
        go(yo, n1, n2, 8, dev_x)
        arrive(my, other, 0, n, 2)
        arrive(ya, other, 0, n, 5)
        arrive(yb, other, 0, n, 6)
        arrive(yo, other, 0, n1, 7)
        arrive(yo, other, n1, n2, 8)
        return sent

    def send2(h):
        def one(o):
            halo1(h, o).wait_send()
            for j in range(CAP):
                stage[h, o, j] = ptab[h, held(asked[o, 0, 0, o * CAP + j], rows)]
            halo2(h, o).start()

        each_peer(one)

    for h in range(2):
        remote_smooth(h)
        sent = make_prolong(h)
        send2(h)
        for copy in sent:
            copy.wait_send()

    def whole(row):
        return jnp.concatenate([ptab[0, row], ptab[1, row]], axis=0)

    def galerkin(slot, tile):
        applied = dot_nt(tile, blocks[slot]).astype(BF16)
        return dot_nt(applied, whole(lax.div(slot, 3)))

    group = 4

    def local_galerkin(b, acc):
        parts = []
        for u in range(group):
            q = b * group + u
            code = tab[7 + q // 128, q % 128]
            parts.append((code >> 15, galerkin(held(code & 255, slots - 1), whole(held((code >> 8) & 127, rows)))))
        for u, (keep, c) in enumerate(parts):
            acc = jnp.where(keep > 0, acc, 0.0) + c
            big[b * group + u] = acc.reshape(2, HALF, 128)
        return acc

    lax.fori_loop(0, n_local // group, local_galerkin, jnp.zeros((128, 128), F32))

    n_out = NCD * KC // (2 * NY)

    def finish(h):
        def one(o):
            halo2(h, o).wait_recv()
            for j in range(CAP):
                big[c_base + o * CAP + j, h] = galerkin(
                    held(tab[6, o * CAP + j], slots - 1), recv2[h, o, j]
                )

        each_peer(one)

        def remote_sum(q, acc):
            code = tab[9, q]
            acc = jnp.where((code >> 15) > 0, acc, 0.0) + big[c_base + held(code & 127, space_count * CAP - 1), h]
            big[g_base + q, h] = acc
            return acc

        lax.fori_loop(0, n_remote, remote_sum, jnp.zeros((HALF, 128), F32), unroll=4)

    for h in range(2):
        finish(h)

    def coarse_part(r):
        t, h = r // 2, r % 2
        end = big.shape[0] - 1
        return big[held(tab[10, t], end), h] + big[held(tab[11, t], end), h]

    drain = reduce_scatter(
        2 * n_out, coarse_part, xs_f, xr_f, s1_f, r1_f, s2_f, r2_f, rf_send, rf_recv, 0
    )
    for t in range(n_out):
        at = 6 * n_out + 2 * t
        out[t] = jnp.concatenate([total[at], total[at + 1]], axis=0).T
    for h in range(2):
        each_peer(lambda o: halo2(h, o).wait_send())
    drain()


def ring_rank(delta, size):
    return jnp.where(delta == 0, 0, jnp.where(2 * delta <= size, 2 * delta - 1, 2 * (size - delta)))


def per_device(
    blocks, basis_tiles, weights, neighbour_device, neighbour_row, counts, aggregate, pair_slot
):
    own = lax.axis_index("space")
    col = lax.axis_index("col")
    space_count = lax.axis_size("space")
    rows, slot_count = neighbour_device.shape
    slots = rows * slot_count
    n_remote = 60
    n_local = slots - n_remote
    live = (
        col * slot_count + jnp.arange(slot_count, dtype=jnp.int32)[None, :] < counts[:, None]
    )
    target = aggregate[:, None] * KC + pair_slot
    step = ring_rank((own % NZ - neighbour_device % NZ) % NZ, NZ) * NX + ring_rank(
        (own // NZ - neighbour_device // NZ) % NX, NX
    )
    fields = jnp.concatenate(
        [step, neighbour_row, target, live.astype(jnp.int32)], axis=1
    )
    fields = jnp.pad(
        fields, ((0, 128 - rows), (0, 128 - 4 * slot_count)), constant_values=-1
    )
    own_rows = rows // (2 * NY)
    n_out = NCD * KC // (2 * NY)
    tile = (128, 128)
    half = (HALF, 128)

    def rs_buffers(lead, n, kind):
        return [pltpu.VMEM(lead + (m * n,) + half, kind) for m in (4, 4, 2, 2, 1, 1)]

    dma = pltpu.SemaphoreType.DMA
    return pl.pallas_call(
        functools.partial(kernel, (rows, slots, n_local)),
        out_shape=jax.ShapeDtypeStruct((n_out,) + tile, F32),
        in_specs=[
            pl.BlockSpec(memory_space=pltpu.VMEM),
            pl.BlockSpec(memory_space=pltpu.VMEM),
            pl.BlockSpec(memory_space=pl.ANY),
            pl.BlockSpec(memory_space=pl.ANY),
        ],
        out_specs=pl.BlockSpec(memory_space=pltpu.VMEM),
        scratch_shapes=[
            pltpu.VMEM((slots,) + tile, BF16),
            pltpu.VMEM((rows,) + tile, BF16),
            pltpu.VMEM((rows + 1, 2) + half, BF16),
            pltpu.VMEM((2, rows + 1) + half, BF16),
            pltpu.VMEM((1, 1, 128), jnp.int32),
            pltpu.VMEM((16, 128), jnp.int32),
            pltpu.SMEM((16, 128), jnp.int32),
            pltpu.VMEM((space_count, 1, 1, 128), jnp.int32),
            pltpu.SMEM((space_count, 1, 1, 128), jnp.int32),
            pltpu.VMEM((2, space_count, CAP) + half, BF16),
            pltpu.VMEM((2, space_count, CAP) + half, BF16),
            pltpu.VMEM((2, space_count, CAP) + half, BF16),
            pltpu.VMEM((n_local + space_count * CAP + n_remote, 2) + half, F32),
            pltpu.VMEM((4 * own_rows,) + half, F32),
            *rs_buffers((), own_rows, S_WIRE),
            *rs_buffers((), 2 * n_out, C_WIRE),
            dma((4,)),
            *([dma((space_count,))] * 2),
            *([dma((2 * space_count,))] * 4),
            *([dma((20,))] * 4),
            *([dma((18,))] * 2),
        ],
        compiler_params=pltpu.CompilerParams(
            collective_id=0, has_side_effects=True, vmem_limit_bytes=62 << 20
        ),
        name="galerkin_step",
    )(
        fields,
        weights.reshape(rows, 1, 128),
        blocks.reshape((slots,) + tile),
        basis_tiles,
    )


def solution(mesh):
    return jax.shard_map(
        per_device,
        mesh=mesh,
        in_specs=(
            P("space", "col", None, None),
            P("space", None, None),
            P("space", None),
            P("space", "col"),
            P("space", "col"),
            P("space"),
            P("space"),
            P("space", "col"),
        ),
        out_specs=P(("space", "col"), None, None),
        check_vma=False,
    )
```
